256 devices in a mesh: region: 4 (over y_hi, core), block: 64 (over y_lo, z, x).
Axes of the slice: x: 4, y: 4 (y_hi: 2, y_lo: 2; y = y_hi * 2 + y_lo), z: 8, core: 2. Of those that a mesh axis runs over, the one named last changes fastest.
Arguments:
- features: bfloat16 [196608, 128], P(('region', 'block')), may hold values from -6 to 6
- grad_out: bfloat16 [196608, 128], P(('region', 'block')), may hold values from -6 to 6
- w1: bfloat16 [27, 128, 128], replicated, may hold values from -0.109375 to 0.109375
- w2: bfloat16 [27, 128, 128], replicated, may hold values from -0.109375 to 0.109375
- rulebook: int32 [27, 196608], P(None, ('region', 'block')), may hold values from 0 to 1024, as said below
- live_blocks: int32 [1536], P(('region', 'block')), may hold values from 0 to 1, as said below
Outputs:
- grad_in: bfloat16 [196608, 128], P(('region', 'block'))
- grad_w1: float32 [27, 128, 128], replicated
- grad_w2: float32 [27, 128, 128], replicated
The draws below stay inside these ranges and needn't reach their ends.
Inputs may be any that keep to these rules, and one draw needn't show every extreme that they name: `rulebook`: entries index slab s's extended rows as in the reference program; the value 768 + 2 * 128 means no neighbour. Every entry of a padded row has that value; no entry points at a padded row or at a missing neighbour; offset 27 // 2 of a live row points at the row itself. An entry of row v of slab s other than 1024 lies between v - s * 768 and v - s * 768 + 2 * 128. `live_blocks`: the first 1 and the last 1 block of every slab are live; the padded blocks of a slab lie between them. Some slab has all 6 blocks live and some slab only 2.
All inputs are finite; a program needn't handle non-finite values.
Results may differ from the reference program's by a relative error of at most 0.0039.
Values may be sent and summed in bfloat16 or wider, within the bound.
No kernel may reach another device: no remote copies, remote signals or barrier semaphores. Data moves between devices by JAX's collectives and lax.ppermute only.
A program may use at most 64 MiB of HBM per device.

```python
import jax
import jax.numpy as jnp
from jax import lax

C = 128
K = 27
BLOCK = 128
NB = 6
HB = 1
ROWS_DEV = 768
HALO = 128
SLABS = 64
VOXELS = 196608


def slab_layout(key):
    base = jax.random.fold_in(key, 4711)
    key_count, key_shift, key_keep = jax.random.split(base, 3)
    slab_count = VOXELS // ROWS_DEV
    counts = jax.random.randint(key_count, (slab_count,), 2 * HB, NB + 1)
    counts = counts.at[0].set(NB).at[1].set(2 * HB)
    block_ids = jnp.arange(NB)
    live = (block_ids[None, :] < counts[:, None] - HB) | (block_ids[None, :] >= NB - HB)
    live = live.astype(jnp.int32)
    row_live = jnp.repeat(live, BLOCK, axis=1)
    shifts = jax.random.randint(key_shift, (K, slab_count, ROWS_DEV), -HALO, HALO + 1)
    center = (jnp.arange(K) == K // 2)[:, None, None]
    shifts = jnp.where(center, 0, shifts)
    keeper = (jax.random.randint(key_keep, (K, slab_count, ROWS_DEV), 0, 4) > 0) | center
    target = jnp.arange(ROWS_DEV)[None, None, :] + shifts
    position = (jnp.arange(slab_count) % SLABS)[None, :, None]
    inside = ((target >= 0) | (position > 0)) & ((target < ROWS_DEV) | (position < SLABS - 1))
    clipped = jnp.clip(target, 0, ROWS_DEV - 1)
    target_live = jnp.take_along_axis(jnp.broadcast_to(row_live[None], (K, slab_count, ROWS_DEV)), clipped, axis=2)
    target_live = jnp.where((target >= 0) & (target < ROWS_DEV), target_live, 1)
    usable = keeper & inside & (target_live == 1) & (row_live[None] == 1)
    rule_table = jnp.where(usable, target + HALO, ROWS_DEV + 2 * HALO).astype(jnp.int32)
    return (rule_table.reshape(K, slab_count * ROWS_DEV), live.reshape(slab_count * NB))


def draw_rulebook(key, part):
    return slab_layout(key)[0]


def draw_live_blocks(key, part):
    return slab_layout(key)[1]


def level_of(key, dims, cuts, least, largest):
    def one(dim, parts):
        heights = jax.random.uniform(jax.random.fold_in(jax.random.fold_in(key, 6), dim), (parts,), jnp.float32, least / len(cuts), largest / len(cuts))
        return jnp.repeat(jnp.exp(heights), dims[dim] // parts).reshape((-1,) + (1,) * (len(dims) - dim - 1))

    factor_of = one(*cuts[0])
    for cut in cuts[1:]:
        factor_of = factor_of * one(*cut)
    return factor_of


def scatter_about(stream_key, dims, deviation, reach, cuts=(), held_as=jnp.bfloat16):
    drawn = deviation * jax.random.normal(stream_key, dims, jnp.float32)
    if cuts:
        drawn = drawn * level_of(stream_key, dims, cuts, -0.22, 0.18)
    return jnp.clip(drawn, -reach, reach).astype(held_as)


def setup_inputs(seed: int = 0) -> dict:
    key_of = jax.random.split(jax.random.key(seed), 7)
    return {
        "features": scatter_about(key_of[0], (VOXELS, C), 1.0, 6.0, ((0, 256),)),
        "grad_out": scatter_about(key_of[1], (VOXELS, C), 1.0, 6.0, ((0, 256),)),
        "w1": scatter_about(key_of[2], (K, C, C), (K * C) ** -0.5, 0.109375),
        "w2": scatter_about(key_of[3], (K, C, C), (K * C) ** -0.5, 0.109375),
        "rulebook": draw_rulebook(jax.random.fold_in(key_of[6], 71), 0),
        "live_blocks": draw_live_blocks(jax.random.fold_in(key_of[6], 71), 0),
    }


def dsilu(hidden):
    sigma = jax.nn.sigmoid(hidden)
    return sigma * (1.0 + hidden * (1.0 - sigma))

def extend(values):
    slab_count = values.shape[0]
    chans = values.shape[2]
    position = jnp.arange(slab_count) % SLABS
    rim_zeros = jnp.zeros((1, HALO, chans), values.dtype)
    before = jnp.concatenate([rim_zeros, values[:-1, ROWS_DEV - HALO:]], 0)
    before = jnp.where((position > 0)[:, None, None], before, jnp.zeros_like(before))
    after = jnp.concatenate([values[1:, :HALO], rim_zeros], 0)
    after = jnp.where((position < SLABS - 1)[:, None, None], after, jnp.zeros_like(after))
    blank = jnp.zeros((slab_count, 1, chans), values.dtype)
    return jnp.concatenate([before, values, after, blank], 1)

def gather_rows(extended, lookup):
    return jax.vmap(lambda source, picks: source[picks])(extended, lookup)

def fold_back(scattered):
    slab_count = scattered.shape[0]
    chans = scattered.shape[2]
    position = jnp.arange(slab_count) % SLABS
    own_rows = scattered[:, HALO:HALO + ROWS_DEV]
    lower_rim = scattered[:, :HALO]
    upper_rim = scattered[:, HALO + ROWS_DEV:2 * HALO + ROWS_DEV]
    rim_zeros = jnp.zeros((1, HALO, chans), scattered.dtype)
    from_above = jnp.concatenate([lower_rim[1:], rim_zeros], 0)
    from_above = jnp.where((position < SLABS - 1)[:, None, None], from_above, jnp.zeros_like(from_above))
    from_below = jnp.concatenate([rim_zeros, upper_rim[:-1]], 0)
    from_below = jnp.where((position > 0)[:, None, None], from_below, jnp.zeros_like(from_below))
    own_rows = own_rows.at[:, :HALO].add(from_below)
    own_rows = own_rows.at[:, ROWS_DEV - HALO:].add(from_above)
    return own_rows

def reference(features, grad_out, w1, w2, rulebook, live_blocks):
    slab_count = VOXELS // ROWS_DEV
    rule_table = rulebook.reshape(K, slab_count, ROWS_DEV)
    ext_feat = extend(features.reshape(slab_count, ROWS_DEV, C))

    def forward(running, pair):
        weight, lookup = pair
        picked = gather_rows(ext_feat, lookup).reshape(-1, C)
        return (running + jnp.dot(picked, weight, preferred_element_type=jnp.float32), None)
    hidden, _ = lax.scan(forward, jnp.zeros((VOXELS, C), jnp.float32), (w1, rule_table))
    act = jax.nn.silu(hidden).astype(jnp.bfloat16)
    ext_act = extend(act.reshape(slab_count, ROWS_DEV, C))
    scale = jnp.sqrt(jnp.float32(VOXELS))

    def kernel_grad(extended, right_side):

        def step(running, lookup):
            picked = gather_rows(extended, lookup).reshape(-1, C)
            return (running, jnp.dot(picked.T, right_side, preferred_element_type=jnp.float32))
        _, grads = lax.scan(step, jnp.zeros((), jnp.float32), rule_table)
        return grads / scale

    def scatter_back(source, weights):
        start = jnp.zeros((slab_count, ROWS_DEV + 2 * HALO + 1, C), jnp.float32)

        def step(running, pair):
            weight, lookup = pair
            spread = jnp.dot(source, weight.T, preferred_element_type=jnp.float32).reshape(slab_count, ROWS_DEV, C)
            added = jax.vmap(lambda target, picks, terms: target.at[picks].add(terms))(running, lookup, spread)
            return (added, None)
        scattered, _ = lax.scan(step, start, (weights, rule_table))
        return fold_back(scattered).reshape(VOXELS, C)
    grad_w2 = kernel_grad(ext_act, grad_out)
    grad_act = scatter_back(grad_out, w2)
    grad_hidden = (grad_act * dsilu(hidden)).astype(jnp.bfloat16)
    grad_w1 = kernel_grad(ext_feat, grad_hidden)
    grad_feat = scatter_back(grad_hidden, w1)
    live = jnp.repeat(live_blocks, BLOCK).astype(jnp.float32)[:, None]
    grad_in = (live * (grad_out.astype(jnp.float32) + grad_feat)).astype(jnp.bfloat16)
    return (grad_in, grad_w1, grad_w2)
```

```python
import jax
import jax.numpy as jnp
from jax import lax
from jax.sharding import Mesh, PartitionSpec as P

BLOCK = 128
HB = 1
HALO = 128


def shifted(x, axis, by):
    length = lax.axis_size(axis)
    pairs = [(i, i + by) for i in range(length) if 0 <= i + by < length]
    return lax.ppermute(x, axis, pairs)


def with_halo(x, sides, width):
    for axis, dim in sides:
        size, length = (lax.axis_size(axis), x.shape[dim])
        up = [(i, (i + 1) % size) for i in range(size - 1)]
        down = [(j, i) for i, j in up]
        last = lax.slice_in_dim(x, length - width, length, axis=dim)
        first = lax.slice_in_dim(x, 0, width, axis=dim)
        before = lax.ppermute(last, axis, up)
        after = lax.ppermute(first, axis, down)
        x = jnp.concatenate([before, x, after], axis=dim)
    return x


SWAP = [(0, 1), (1, 0)]
PLANE = ("yh", "yl", "x")
BLOCKS = ("yl", "z", "x")
REGIONS = ("yh", "core")


def fine_mesh(mesh):
    return Mesh(mesh.devices.reshape(2, 2, 2, 8, 4), ("yh", "core", "yl", "z", "x"))


def reduce_everywhere(x):
    core = lax.axis_index("core")
    halves = x.reshape(2, -1, x.shape[1])
    own = lax.dynamic_index_in_dim(halves, core, 0, False)
    other = lax.dynamic_index_in_dim(halves, 1 - core, 0, False)
    own = own + lax.ppermute(other.astype(jnp.bfloat16), "core", SWAP).astype(jnp.float32)
    count = lax.axis_size(PLANE)
    parts = own.astype(jnp.bfloat16).reshape(count, -1, x.shape[1])
    parts = lax.all_to_all(parts, PLANE, 0, 0, tiled=True)
    own = parts.astype(jnp.float32).sum(0)
    size = lax.axis_size("z")
    hop = 1
    while hop < size:
        own = own + lax.ppermute(own, "z", [(i, i ^ hop) for i in range(size)])
        hop *= 2
    parts = jnp.broadcast_to(own.astype(jnp.bfloat16)[None], (count,) + own.shape)
    parts = lax.all_to_all(parts, PLANE, 0, 0, tiled=True).reshape(-1, x.shape[1])
    other = lax.ppermute(parts, "core", SWAP)
    low = jnp.where(core == 0, parts, other)
    high = jnp.where(core == 0, other, parts)
    return jnp.concatenate([low, high], 0).astype(jnp.float32)


def dsilu(hidden):
    sigma = jax.nn.sigmoid(hidden)
    return sigma * (1.0 + hidden * (1.0 - sigma))


def give_back(scattered, row_count, halo_rows):
    own_rows = scattered[halo_rows : halo_rows + row_count]
    lower_rim = scattered[:halo_rows]
    upper_rim = scattered[halo_rows + row_count : 2 * halo_rows + row_count]
    from_above = shifted(lower_rim.astype(jnp.bfloat16), BLOCKS, -1).astype(lower_rim.dtype)
    from_below = shifted(upper_rim.astype(jnp.bfloat16), BLOCKS, 1).astype(upper_rim.dtype)
    own_rows = own_rows.at[:halo_rows].add(from_below)
    return own_rows.at[row_count - halo_rows :].add(from_above)


def on_device(features, grad_out, w1, w2, rulebook, live_blocks):
    row_count, chans = features.shape
    offsets = w1.shape[0]
    halo_rows = HALO
    block_rows = BLOCK
    block_count = row_count // block_rows
    span_blocks = 1 + 2 * HB
    window = span_blocks * block_rows
    offset_group = 9
    group_starts = list(range(0, offsets, offset_group))
    block_base = (jnp.arange(block_count, dtype=jnp.int32) * block_rows)[None, :, None]
    window_ids = jnp.arange(window, dtype=jnp.int32)

    def selector(first):
        lookup = rulebook[first : first + offset_group].reshape(
            offset_group, block_count, block_rows
        )
        local_index = lookup - block_base
        return (local_index[..., None] == window_ids).astype(jnp.bfloat16)

    selectors = [selector(first) for first in group_starts]

    def windows(extended):
        blocks = extended.reshape(block_count + 2 * HB, block_rows, chans)
        return jnp.concatenate([blocks[j : j + block_count] for j in range(span_blocks)], 1)

    def picked_rows(select, framed):
        picked = jnp.einsum("gbiw,bwc->gbic", select, framed, preferred_element_type=jnp.float32)
        return picked.astype(jnp.bfloat16)

    def kernel_grad(framed, right_side):
        right_blocks = right_side.reshape(block_count, block_rows, chans)
        pieces = []
        for select in selectors:
            picked = picked_rows(select, framed)
            pieces.append(
                jnp.einsum(
                    "gbic,bid->gcd", picked, right_blocks, preferred_element_type=jnp.float32
                )
            )
        return jnp.concatenate(pieces, 0)

    def scatter_back(source, weights):
        source_blocks = source.reshape(block_count, block_rows, chans)
        framed_sum = jnp.zeros((block_count, window, chans), jnp.float32)
        for select, first in zip(selectors, group_starts):
            spread = jnp.einsum(
                "bid,gcd->gbic",
                source_blocks,
                weights[first : first + offset_group],
                preferred_element_type=jnp.float32,
            )
            framed_sum = framed_sum + jnp.einsum(
                "gbiw,gbic->bwc",
                select.astype(jnp.float32),
                spread,
                precision=lax.Precision.HIGHEST,
                preferred_element_type=jnp.float32,
            )
        framed_sum = framed_sum.reshape(block_count, span_blocks, block_rows, chans)
        folded = jnp.zeros((block_count + 2 * HB, block_rows, chans), jnp.float32)
        for j in range(span_blocks):
            folded = folded + jnp.pad(framed_sum[:, j], ((j, span_blocks - 1 - j), (0, 0), (0, 0)))
        return give_back(folded.reshape(-1, chans), row_count, halo_rows)

    ext_feat = with_halo(features, ((BLOCKS, 0),), halo_rows)
    framed_feat = windows(ext_feat)
    hidden_blocks = jnp.zeros((block_count, block_rows, chans), jnp.float32)
    for select, first in zip(selectors, group_starts):
        picked = picked_rows(select, framed_feat)
        hidden_blocks = hidden_blocks + jnp.einsum(
            "gbic,gcd->bid",
            picked,
            w1[first : first + offset_group],
            preferred_element_type=jnp.float32,
        )
    hidden = hidden_blocks.reshape(row_count, chans)
    act = jax.nn.silu(hidden).astype(jnp.bfloat16)
    ext_act = with_halo(act, ((BLOCKS, 0),), halo_rows)
    framed_act = windows(ext_act)
    kern_two = kernel_grad(framed_act, grad_out)
    grad_act = scatter_back(grad_out, w2)
    grad_hidden = (grad_act * dsilu(hidden)).astype(jnp.bfloat16)
    kern_one = kernel_grad(framed_feat, grad_hidden)
    grad_feat = scatter_back(grad_hidden, w1)
    both = jnp.concatenate([kern_one.reshape(-1, chans), kern_two.reshape(-1, chans)], 0)
    both = reduce_everywhere(both).reshape((2,) + kern_one.shape)
    kern_one, kern_two = (both[0], both[1])
    voxel_total = row_count * lax.axis_size(REGIONS) * lax.axis_size(BLOCKS)
    scale = jnp.sqrt(jnp.float32(voxel_total))
    live = jnp.repeat(live_blocks, block_rows).astype(jnp.float32)[:, None]
    grad_in = (live * (grad_out.astype(jnp.float32) + grad_feat)).astype(jnp.bfloat16)
    return (grad_in, kern_one / scale, kern_two / scale)


def solution(mesh):
    rows = P(REGIONS + BLOCKS)
    return jax.shard_map(
        on_device,
        mesh=fine_mesh(mesh),
        in_specs=(rows, rows, P(), P(), P(None, REGIONS + BLOCKS), rows),
        out_specs=(rows, P(), P()),
        check_vma=False,
    )
```

```python
import jax
import jax.numpy as jnp
from jax import lax
from jax.experimental import pallas as pl
from jax.experimental.pallas import tpu as pltpu
from jax.sharding import Mesh, PartitionSpec as P

BLOCK = 128
HALO = 128
SPAN = 256
EDGE = 256
CODE = 32
NONE = 4096
GROUP = 3


def shifted(x, axis, by):
    length = lax.axis_size(axis)
    pairs = [(i, i + by) for i in range(length) if 0 <= i + by < length]
    return lax.ppermute(x, axis, pairs)


SWAP = [(0, 1), (1, 0)]
PLANE = ("yh", "yl", "x")
BLOCKS = ("yl", "z", "x")
REGIONS = ("yh", "core")


def fine_mesh(mesh):
    return Mesh(mesh.devices.reshape(2, 2, 2, 8, 4), ("yh", "core", "yl", "z", "x"))


def reduce_everywhere(own, other):
    core = lax.axis_index("core")
    lanes = own.shape[1]
    own = own + lax.ppermute(other, "core", SWAP).astype(jnp.float32)
    count = lax.axis_size(PLANE)
    parts = own.astype(jnp.bfloat16).reshape(count, -1, lanes)
    parts = lax.all_to_all(parts, PLANE, 0, 0, tiled=True)
    own = parts.astype(jnp.float32).sum(0)
    size = lax.axis_size("z")
    for flip in (1, 2, 7):
        own = own + lax.ppermute(own, "z", [(i, i ^ flip) for i in range(size)])
    parts = jnp.broadcast_to(own.astype(jnp.bfloat16)[None], (count,) + own.shape)
    parts = lax.all_to_all(parts, PLANE, 0, 0, tiled=True).reshape(-1, lanes)
    other = lax.ppermute(parts, "core", SWAP)
    first = jnp.where(core == 0, parts, other)
    second = jnp.where(core == 0, other, parts)
    return first.astype(jnp.float32), second.astype(jnp.float32)


def dsilu(hidden):
    sigma = jax.nn.sigmoid(hidden)
    return sigma * (1.0 + hidden * (1.0 - sigma))


def fill_ids(ids_ref):
    ids_ref[...] = lax.broadcasted_iota(jnp.int32, ids_ref.shape, 0).astype(jnp.float32).astype(jnp.bfloat16)


def one_hot(ids_ref, entries):
    place = (entries & (SPAN - 1)).astype(jnp.float32).astype(jnp.bfloat16)
    return jnp.where(ids_ref[...] == place, jnp.ones((), jnp.bfloat16), jnp.zeros((), jnp.bfloat16))


def over_offsets(offsets, chans, step):
    def group(index, carry):
        for inner in range(GROUP):
            k = index * GROUP + inner
            step(k, pl.ds(pl.multiple_of(k * chans, chans), chans))
        return carry

    lax.fori_loop(0, offsets // GROUP, group, 0)


def gather_into(picked_ref, rule_ref, ids_ref, tiles, offsets, start, shift):
    chans = tiles[0].shape[0]
    sides = [jnp.concatenate([a, b], 0) for a, b in zip(tiles[:-1], tiles[1:])]

    def step(k, at):
        for q, side in enumerate(sides):
            entries = rule_ref[pl.ds(k, 1), start + SPAN * q : start + SPAN * (q + 1)] - shift
            both = jnp.dot(side, one_hot(ids_ref, entries), preferred_element_type=jnp.float32)
            half = lax.shift_right_arithmetic(entries, 8)
            found = jnp.where(half == q, both[:chans], jnp.where(half == q + 1, both[chans:], 0.0))
            picked_ref[at, SPAN * q : SPAN * (q + 1)] = found.astype(jnp.bfloat16)

    over_offsets(offsets, chans, step)


def side_by_side(w_ref, out_ref, turned):
    offsets, chans, _ = w_ref.shape
    for k in range(offsets):
        out_ref[:, k * chans : (k + 1) * chans] = w_ref[k].T if turned else w_ref[k]


def scatter_to(high_ref, low_ref, rule_ref, ids_ref, sources, w_ref, offsets, start, shift):
    chans = sources[0].shape[0]
    last = len(sources) - 1

    def put(at, q, tile):
        first = tile.astype(jnp.bfloat16)
        high_ref[at, SPAN * q : SPAN * (q + 1)] = first
        low_ref[at, SPAN * q : SPAN * (q + 1)] = (tile - first.astype(jnp.float32)).astype(jnp.bfloat16)

    def step(k, at):
        above = None
        for q, source in enumerate(sources):
            entries = rule_ref[pl.ds(k, 1), start + SPAN * q : start + SPAN * (q + 1)] + shift
            half = lax.shift_right_arithmetic(entries, 8)
            none = jnp.zeros((), jnp.bfloat16)
            parts = [] if q == 0 else [jnp.where(half == q, source, none)]
            if q < last:
                parts.append(jnp.where(half == q + 1, source, none))
            spread = lax.dot_general(
                jnp.concatenate(parts, 0) if len(parts) > 1 else parts[0],
                one_hot(ids_ref, entries),
                (((1,), (1,)), ((), ())),
                preferred_element_type=jnp.float32,
            )
            if q > 0:
                put(at, q - 1, above + spread[:chans])
            above = spread[-chans:]

    over_offsets(offsets, chans, step)
    used = SPAN * last
    total = jnp.dot(w_ref[...], high_ref[:, :used], preferred_element_type=jnp.float32)
    return total + jnp.dot(w_ref[...], low_ref[:, :used], preferred_element_type=jnp.float32)


def pack_kernel(feat_ref, grad_ref, rule_ref, own_ref, first_ref, last_ref):
    rows, chans = feat_ref.shape
    offsets = rule_ref.shape[0]
    own_ref[2 * chans :, :] = jnp.zeros((2 * CODE, rows), jnp.bfloat16)
    for b in range(rows // BLOCK):
        at = slice(b * BLOCK, (b + 1) * BLOCK)
        own_ref[:chans, at] = feat_ref[at, :].T
        own_ref[chans : 2 * chans, at] = grad_ref[at, :].T
    entries = rule_ref[...]
    code = jnp.where(entries == rows + 2 * HALO, 0, entries + 1)
    coarse = lax.shift_right_logical(code, 5).astype(jnp.float32).astype(jnp.bfloat16)
    fine = (code & 31).astype(jnp.float32).astype(jnp.bfloat16)
    own_ref[2 * chans : 2 * chans + offsets, :] = coarse
    own_ref[2 * chans + CODE : 2 * chans + CODE + offsets, :] = fine
    first_ref[...] = own_ref[:, :EDGE]
    last_ref[...] = own_ref[:, rows - EDGE :]


def grads_kernel(
    own_ref, before_ref, after_ref, grad_out_ref, w1_ref, w2_ref, core_ref,
    mine_ref, other_ref, source_ref, rule_ref,
    high_ref, low_ref, picked_ref, w_ref, ids_ref,
):
    rows, chans = grad_out_ref.shape
    offsets = mine_ref.shape[0] // chans
    wide = rows + 2 * HALO
    fill_ids(ids_ref)
    pieces = ((before_ref, -HALO - rows + EDGE), (own_ref, EDGE - HALO), (after_ref, EDGE - HALO + rows))
    column = 0
    for piece, base in pieces:
        coarse = piece[2 * chans : 2 * chans + CODE, :].astype(jnp.float32)
        fine = piece[2 * chans + CODE :, :].astype(jnp.float32)
        code = (coarse * 32.0 + fine).astype(jnp.int32)
        rule_ref[:, column : column + code.shape[1]] = jnp.where(code == 0, NONE, code - 1 + base)
        column += code.shape[1]

    def tiles(top):
        rest = slice(top, top + chans)
        inner = [own_ref[rest, SPAN * p : SPAN * (p + 1)] for p in range(rows // SPAN)]
        return [before_ref[rest, :]] + inner + [after_ref[rest, :]]

    side_by_side(w2_ref, w_ref, False)
    grad_act = scatter_to(
        high_ref, low_ref, rule_ref, ids_ref, tiles(chans), w_ref, offsets, 0, HALO
    )
    side_by_side(w1_ref, w_ref, True)
    gather_into(picked_ref, rule_ref, ids_ref, tiles(0), offsets, HALO, 0)
    hidden = jnp.dot(w_ref[...], picked_ref[...], preferred_element_type=jnp.float32)
    act = (hidden * jax.nn.sigmoid(hidden)).astype(jnp.bfloat16)
    grad_hidden = (grad_act * dsilu(hidden)).astype(jnp.bfloat16)
    source_ref[...] = grad_hidden
    inside = slice(HALO, HALO + rows)
    first = lax.dot_general(
        picked_ref[:, inside], grad_hidden[:, inside], (((1,), (1,)), ((), ())), preferred_element_type=jnp.float32
    )

    @pl.when(core_ref[0] == 0)
    def _():
        mine_ref[...] = first

    @pl.when(core_ref[0] != 0)
    def _():
        other_ref[...] = first.astype(jnp.bfloat16)

    act_tiles = [act[:, SPAN * q : SPAN * (q + 1)] for q in range(wide // SPAN)]
    gather_into(high_ref, rule_ref, ids_ref, act_tiles, offsets, EDGE, EDGE - HALO)
    second = jnp.dot(high_ref[:, :rows], grad_out_ref[...], preferred_element_type=jnp.float32)

    @pl.when(core_ref[0] != 0)
    def _():
        mine_ref[...] = second

    @pl.when(core_ref[0] == 0)
    def _():
        other_ref[...] = second.astype(jnp.bfloat16)


def input_grad_kernel(
    source_ref, rule_ref, w1_ref, grad_out_ref, live_ref, out_ref, high_ref, low_ref, w_ref, ids_ref
):
    rows, _ = grad_out_ref.shape
    offsets = w1_ref.shape[0]
    fill_ids(ids_ref)
    side_by_side(w1_ref, w_ref, False)
    sources = [source_ref[:, SPAN * q : SPAN * (q + 1)] for q in range(source_ref.shape[1] // SPAN)]
    total = scatter_to(high_ref, low_ref, rule_ref, ids_ref, sources, w_ref, offsets, HALO, 0)
    for b in range(rows // BLOCK):
        at = slice(b * BLOCK, (b + 1) * BLOCK)
        added = grad_out_ref[at, :].astype(jnp.float32) + total[:, at].T
        out_ref[at, :] = (live_ref[b].astype(jnp.float32) * added).astype(jnp.bfloat16)


def call(kernel, outs, scratch, *args, scalars=0, flops=0):
    vmem = pl.BlockSpec(memory_space=pltpu.VMEM)
    smem = pl.BlockSpec(memory_space=pltpu.SMEM)
    shapes = [jax.ShapeDtypeStruct(shape, dtype) for shape, dtype in outs]
    moved = sum(x.size * x.dtype.itemsize for x in (*args, *shapes))
    return pl.pallas_call(
        kernel,
        out_shape=shapes,
        in_specs=[vmem] * (len(args) - scalars) + [smem] * scalars,
        out_specs=[vmem] * len(outs),
        scratch_shapes=[pltpu.VMEM(shape, dtype) for shape, dtype in scratch],
        cost_estimate=pl.CostEstimate(flops=flops, bytes_accessed=moved, transcendentals=0),
    )(*args)


def on_device(features, grad_out, w1, w2, rulebook, live_blocks):
    rows, chans = features.shape
    offsets = w1.shape[0]
    wide = rows + 2 * HALO
    flat = offsets * chans
    bf16, f32, i32 = (jnp.bfloat16, jnp.float32, jnp.int32)
    ids = ((SPAN, SPAN), bf16)
    spread = ((flat, wide), bf16)
    beside = ((chans, flat), bf16)
    tall = 2 * chans + 2 * CODE
    one_pass = 2 * offsets * rows * SPAN * SPAN
    own, first, last = call(
        pack_kernel,
        [((tall, rows), bf16), ((tall, EDGE), bf16), ((tall, EDGE), bf16)],
        [],
        features,
        grad_out,
        rulebook,
    )
    before = shifted(last, BLOCKS, 1)
    after = shifted(first, BLOCKS, -1)
    core = lax.axis_index("core").astype(i32).reshape(1)
    mine, other, grad_hidden, wide_rules = call(
        grads_kernel,
        [((flat, chans), f32), ((flat, chans), bf16), ((chans, wide), bf16), ((CODE, rows + 2 * EDGE), i32)],
        [spread, spread, spread, beside, ids],
        own,
        before,
        after,
        grad_out,
        w1,
        w2,
        core,
        scalars=1,
        flops=6 * one_pass,
    )
    (grad_in,) = call(
        input_grad_kernel,
        [((rows, chans), bf16)],
        [((flat, rows), bf16), ((flat, rows), bf16), beside, ids],
        grad_hidden,
        wide_rules,
        w1,
        grad_out,
        live_blocks,
        scalars=1,
        flops=2 * one_pass,
    )
    kern_one, kern_two = reduce_everywhere(mine, other)
    voxel_total = rows * lax.axis_size(REGIONS) * lax.axis_size(BLOCKS)
    scale = jnp.sqrt(jnp.float32(voxel_total))
    return (grad_in, kern_one.reshape(w1.shape) / scale, kern_two.reshape(w1.shape) / scale)


def solution(mesh):
    rows = P(REGIONS + BLOCKS)

    return jax.shard_map(
        on_device,
        mesh=fine_mesh(mesh),
        in_specs=(rows, rows, P(), P(), P(None, REGIONS + BLOCKS), rows),
        out_specs=(rows, P(), P()),
        check_vma=False,
    )
```

```python
import jax
import jax.numpy as jnp
from jax import lax
from jax.experimental import pallas as pl
from jax.experimental.pallas import tpu as pltpu
from jax.sharding import Mesh, PartitionSpec as P

BLOCK = 128
HALO = 128
SPAN = 256
EDGE = 256
CODE = 32
NONE = 4096
GROUP = 9


def swapped(x, axis, odd):
    length = lax.axis_size(axis)
    pairs = [(i, ((i + odd) ^ 1) - odd) for i in range(length)]
    return lax.ppermute(x, axis, [(i, j) for i, j in pairs if 0 <= j < length])


SWAP = [(0, 1), (1, 0)]
PLANE = ("yh", "yl", "z_lo", "x")
BLOCKS = ("yl", "z_hi", "z_lo", "x")
REGIONS = ("yh", "core")


def fine_mesh(mesh):
    return Mesh(mesh.devices.reshape(2, 2, 2, 4, 2, 4), ("yh", "core", "yl", "z_hi", "z_lo", "x"))


def reduce_everywhere(own, other):
    core = lax.axis_index("core")
    lanes = own.shape[1]
    own = own + lax.ppermute(other, "core", SWAP).astype(jnp.float32)
    count = lax.axis_size(PLANE)
    parts = own.astype(jnp.bfloat16).reshape(count, -1, lanes)
    parts = lax.all_to_all(parts, PLANE, 0, 0, tiled=True)
    own = parts.astype(jnp.float32).sum(0)
    for flip in (1, 3):
        own = own + lax.ppermute(own, "z_hi", [(i, i ^ flip) for i in range(lax.axis_size("z_hi"))])
    parts = jnp.broadcast_to(own.astype(jnp.bfloat16)[None], (count,) + own.shape)
    parts = lax.all_to_all(parts, PLANE, 0, 0, tiled=True).reshape(-1, lanes)
    other = lax.ppermute(parts, "core", SWAP)
    first = jnp.where(core == 0, parts, other)
    second = jnp.where(core == 0, other, parts)
    return first.astype(jnp.float32), second.astype(jnp.float32)


def dsilu(hidden):
    sigma = jax.nn.sigmoid(hidden)
    return sigma * (1.0 + hidden * (1.0 - sigma))


def fill_ids(ids_ref):
    ids_ref[...] = lax.broadcasted_iota(jnp.int32, ids_ref.shape, 0).astype(jnp.float32).astype(jnp.bfloat16)


def one_hot(ids_ref, entries):
    place = (entries & (SPAN - 1)).astype(jnp.float32).astype(jnp.bfloat16)
    return jnp.where(ids_ref[...] == place, jnp.ones((), jnp.bfloat16), jnp.zeros((), jnp.bfloat16))


def over_offsets(offsets, chans, step):
    def group(index, carry):
        for inner in range(GROUP):
            k = index * GROUP + inner
            step(k, pl.ds(pl.multiple_of(k * chans, chans), chans))
        return carry

    lax.fori_loop(0, offsets // GROUP, group, 0)


def gather_into(picked_ref, rule_ref, ids_ref, tiles, offsets, start, shift):
    chans = tiles[0].shape[0]
    sides = [jnp.concatenate([a, b], 0) for a, b in zip(tiles[:-1], tiles[1:])]

    def step(k, at):
        for q, side in enumerate(sides):
            entries = rule_ref[pl.ds(k, 1), start + SPAN * q : start + SPAN * (q + 1)] - shift
            both = jnp.dot(side, one_hot(ids_ref, entries), preferred_element_type=jnp.float32)
            half = lax.shift_right_arithmetic(entries, 8)
            found = jnp.where(half == q, both[:chans], jnp.where(half == q + 1, both[chans:], 0.0))
            picked_ref[at, SPAN * q : SPAN * (q + 1)] = found.astype(jnp.bfloat16)

    over_offsets(offsets, chans, step)


def side_by_side(w_ref, out_ref, turned):
    offsets, chans, _ = w_ref.shape
    for k in range(offsets):
        out_ref[:, k * chans : (k + 1) * chans] = w_ref[k].T if turned else w_ref[k]


def scatter_to(high_ref, low_ref, rule_ref, ids_ref, sources, w_ref, offsets, start, shift):
    chans = sources[0].shape[0]
    last = len(sources) - 1

    def put(at, q, tile):
        first = tile.astype(jnp.bfloat16)
        high_ref[at, SPAN * q : SPAN * (q + 1)] = first
        low_ref[at, SPAN * q : SPAN * (q + 1)] = (tile - first.astype(jnp.float32)).astype(jnp.bfloat16)

    def step(k, at):
        above = None
        for q, source in enumerate(sources):
            entries = rule_ref[pl.ds(k, 1), start + SPAN * q : start + SPAN * (q + 1)] + shift
            half = lax.shift_right_arithmetic(entries, 8)
            none = jnp.zeros((), jnp.bfloat16)
            parts = [] if q == 0 else [jnp.where(half == q, source, none)]
            if q < last:
                parts.append(jnp.where(half == q + 1, source, none))
            spread = lax.dot_general(
                jnp.concatenate(parts, 0) if len(parts) > 1 else parts[0],
                one_hot(ids_ref, entries),
                (((1,), (1,)), ((), ())),
                preferred_element_type=jnp.float32,
            )
            if q > 0:
                put(at, q - 1, above + spread[:chans])
            above = spread[-chans:]

    over_offsets(offsets, chans, step)
    used = SPAN * last
    total = jnp.dot(w_ref[...], high_ref[:, :used], preferred_element_type=jnp.float32)
    return total + jnp.dot(w_ref[...], low_ref[:, :used], preferred_element_type=jnp.float32)


def pack_kernel(feat_ref, grad_ref, rule_ref, odd_ref, own_ref, to_even_ref, to_odd_ref):
    rows, chans = feat_ref.shape
    offsets = rule_ref.shape[0]
    own_ref[2 * chans :, :] = jnp.zeros((2 * CODE, rows), jnp.bfloat16)
    for b in range(rows // BLOCK):
        at = slice(b * BLOCK, (b + 1) * BLOCK)
        own_ref[:chans, at] = feat_ref[at, :].T
        own_ref[chans : 2 * chans, at] = grad_ref[at, :].T
    entries = rule_ref[...]
    code = jnp.where(entries == rows + 2 * HALO, 0, entries + 1)
    coarse = lax.shift_right_logical(code, 5).astype(jnp.float32).astype(jnp.bfloat16)
    fine = (code & 31).astype(jnp.float32).astype(jnp.bfloat16)
    own_ref[2 * chans : 2 * chans + offsets, :] = coarse
    own_ref[2 * chans + CODE : 2 * chans + CODE + offsets, :] = fine
    first, last = own_ref[:, :EDGE], own_ref[:, rows - EDGE :]
    odd = odd_ref[0] == 1
    to_even_ref[...] = jnp.where(odd, first, last)
    to_odd_ref[...] = jnp.where(odd, last, first)


def grads_kernel(
    own_ref, even_ref, odd_ref, grad_out_ref, w1_ref, w2_ref, core_ref, parity_ref,
    mine_ref, other_ref, source_ref, rule_ref,
    high_ref, low_ref, picked_ref, w_ref, before_ref, after_ref, ids_ref,
):
    rows, chans = grad_out_ref.shape
    offsets = mine_ref.shape[0] // chans
    wide = rows + 2 * HALO
    fill_ids(ids_ref)
    is_odd = parity_ref[0] == 1
    before_ref[...] = jnp.where(is_odd, even_ref[...], odd_ref[...])
    after_ref[...] = jnp.where(is_odd, odd_ref[...], even_ref[...])
    pieces = ((before_ref, -HALO - rows + EDGE), (own_ref, EDGE - HALO), (after_ref, EDGE - HALO + rows))
    column = 0
    for piece, base in pieces:
        coarse = piece[2 * chans : 2 * chans + CODE, :].astype(jnp.float32)
        fine = piece[2 * chans + CODE :, :].astype(jnp.float32)
        code = (coarse * 32.0 + fine).astype(jnp.int32)
        rule_ref[:, column : column + code.shape[1]] = jnp.where(code == 0, NONE, code - 1 + base)
        column += code.shape[1]

    def tiles(top):
        rest = slice(top, top + chans)
        inner = [own_ref[rest, SPAN * p : SPAN * (p + 1)] for p in range(rows // SPAN)]
        return [before_ref[rest, :]] + inner + [after_ref[rest, :]]

    side_by_side(w2_ref, w_ref, False)
    grad_act = scatter_to(
        high_ref, low_ref, rule_ref, ids_ref, tiles(chans), w_ref, offsets, 0, HALO
    )
    side_by_side(w1_ref, w_ref, True)
    gather_into(picked_ref, rule_ref, ids_ref, tiles(0), offsets, HALO, 0)
    hidden = jnp.dot(w_ref[...], picked_ref[...], preferred_element_type=jnp.float32)
    act = (hidden * jax.nn.sigmoid(hidden)).astype(jnp.bfloat16)
    grad_hidden = (grad_act * dsilu(hidden)).astype(jnp.bfloat16)
    source_ref[...] = grad_hidden
    inside = slice(HALO, HALO + rows)
    first = lax.dot_general(
        picked_ref[:, inside], grad_hidden[:, inside], (((1,), (1,)), ((), ())), preferred_element_type=jnp.float32
    )

    @pl.when(core_ref[0] == 0)
    def _():
        mine_ref[...] = first

    @pl.when(core_ref[0] != 0)
    def _():
        other_ref[...] = first.astype(jnp.bfloat16)

    act_tiles = [act[:, SPAN * q : SPAN * (q + 1)] for q in range(wide // SPAN)]
    gather_into(high_ref, rule_ref, ids_ref, act_tiles, offsets, EDGE, EDGE - HALO)
    second = jnp.dot(high_ref[:, :rows], grad_out_ref[...], preferred_element_type=jnp.float32)

    @pl.when(core_ref[0] != 0)
    def _():
        mine_ref[...] = second

    @pl.when(core_ref[0] == 0)
    def _():
        other_ref[...] = second.astype(jnp.bfloat16)


def input_grad_kernel(
    source_ref, rule_ref, w1_ref, grad_out_ref, live_ref, out_ref, high_ref, low_ref, w_ref, ids_ref
):
    rows, _ = grad_out_ref.shape
    offsets = w1_ref.shape[0]
    fill_ids(ids_ref)
    side_by_side(w1_ref, w_ref, False)
    sources = [source_ref[:, SPAN * q : SPAN * (q + 1)] for q in range(source_ref.shape[1] // SPAN)]
    total = scatter_to(high_ref, low_ref, rule_ref, ids_ref, sources, w_ref, offsets, HALO, 0)
    for b in range(rows // BLOCK):
        at = slice(b * BLOCK, (b + 1) * BLOCK)
        added = grad_out_ref[at, :].astype(jnp.float32) + total[:, at].T
        out_ref[at, :] = (live_ref[b].astype(jnp.float32) * added).astype(jnp.bfloat16)


def call(kernel, outs, scratch, *args, scalars=0, flops=0):
    vmem = pl.BlockSpec(memory_space=pltpu.VMEM)
    smem = pl.BlockSpec(memory_space=pltpu.SMEM)
    shapes = [jax.ShapeDtypeStruct(shape, dtype) for shape, dtype in outs]
    moved = sum(x.size * x.dtype.itemsize for x in (*args, *shapes))
    return pl.pallas_call(
        kernel,
        out_shape=shapes,
        in_specs=[vmem] * (len(args) - scalars) + [smem] * scalars,
        out_specs=[vmem] * len(outs),
        scratch_shapes=[pltpu.VMEM(shape, dtype) for shape, dtype in scratch],
        cost_estimate=pl.CostEstimate(flops=flops, bytes_accessed=moved, transcendentals=0),
    )(*args)


def on_device(features, grad_out, w1, w2, rulebook, live_blocks):
    rows, chans = features.shape
    offsets = w1.shape[0]
    wide = rows + 2 * HALO
    flat = offsets * chans
    bf16, f32, i32 = (jnp.bfloat16, jnp.float32, jnp.int32)
    ids = ((SPAN, SPAN), bf16)
    spread = ((flat, wide), bf16)
    beside = ((chans, flat), bf16)
    tall = 2 * chans + 2 * CODE
    one_pass = 2 * offsets * rows * SPAN * SPAN
    parity = (lax.axis_index("x").astype(i32) & 1).reshape(1)
    own, to_even, to_odd = call(
        pack_kernel,
        [((tall, rows), bf16), ((tall, EDGE), bf16), ((tall, EDGE), bf16)],
        [],
        features,
        grad_out,
        rulebook,
        parity,
        scalars=1,
    )
    even = swapped(to_even, BLOCKS, 0)
    odd = swapped(to_odd, BLOCKS, 1)
    core = lax.axis_index("core").astype(i32).reshape(1)
    mine, other, grad_hidden, wide_rules = call(
        grads_kernel,
        [((flat, chans), f32), ((flat, chans), bf16), ((chans, wide), bf16), ((CODE, rows + 2 * EDGE), i32)],
        [spread, spread, spread, beside, ((tall, EDGE), bf16), ((tall, EDGE), bf16), ids],
        own,
        even,
        odd,
        grad_out,
        w1,
        w2,
        core,
        parity,
        scalars=2,
        flops=6 * one_pass,
    )
    (grad_in,) = call(
        input_grad_kernel,
        [((rows, chans), bf16)],
        [((flat, rows), bf16), ((flat, rows), bf16), beside, ids],
        grad_hidden,
        wide_rules,
        w1,
        grad_out,
        live_blocks,
        scalars=1,
        flops=2 * one_pass,
    )
    kern_one, kern_two = reduce_everywhere(mine, other)
    voxel_total = rows * lax.axis_size(REGIONS) * lax.axis_size(BLOCKS)
    scale = jnp.sqrt(jnp.float32(voxel_total))
    return (grad_in, kern_one.reshape(w1.shape) / scale, kern_two.reshape(w1.shape) / scale)


def solution(mesh):
    rows = P(REGIONS + BLOCKS)

    return jax.shard_map(
        on_device,
        mesh=fine_mesh(mesh),
        in_specs=(rows, rows, P(), P(), P(None, REGIONS + BLOCKS), rows),
        out_specs=(rows, P(), P()),
        check_vma=False,
    )
```

```python
import jax
import jax.numpy as jnp
from jax import lax
from jax.experimental import pallas as pl
from jax.experimental.pallas import tpu as pltpu
from jax.sharding import Mesh, PartitionSpec as P

BLOCK = 128
HALO = 128
SPAN = 256
EDGE = 256
CODE = 32
NONE = 4096
GROUP = 9
LONG = 9


def swapped(x, axis, odd):
    length = lax.axis_size(axis)
    pairs = [(i, ((i + odd) ^ 1) - odd) for i in range(length)]
    return lax.ppermute(x, axis, [(i, j) for i, j in pairs if 0 <= j < length])


SWAP = [(0, 1), (1, 0)]
PLANE = ("yh", "yl", "z_lo", "x")
BLOCKS = ("yl", "z_hi", "z_lo", "x")
REGIONS = ("yh", "core")


def fine_mesh(mesh):
    return Mesh(mesh.devices.reshape(2, 2, 2, 4, 2, 4), ("yh", "core", "yl", "z_hi", "z_lo", "x"))


def reduce_everywhere(own, other):
    core = lax.axis_index("core")
    lanes = own.shape[1]
    own = own + lax.ppermute(other, "core", SWAP).astype(jnp.float32)
    count = lax.axis_size(PLANE)
    parts = own.astype(jnp.bfloat16).reshape(count, -1, lanes)
    parts = lax.all_to_all(parts, PLANE, 0, 0, tiled=True)
    own = parts.astype(jnp.float32).sum(0)
    for flip in (1, 3):
        own = own + lax.ppermute(own, "z_hi", [(i, i ^ flip) for i in range(lax.axis_size("z_hi"))])
    parts = jnp.broadcast_to(own.astype(jnp.bfloat16)[None], (count,) + own.shape)
    parts = lax.all_to_all(parts, PLANE, 0, 0, tiled=True).reshape(-1, lanes)
    other = lax.ppermute(parts, "core", SWAP)
    first = jnp.where(core == 0, parts, other)
    second = jnp.where(core == 0, other, parts)
    return first.astype(jnp.float32), second.astype(jnp.float32)


def dsilu(hidden):
    sigma = jax.nn.sigmoid(hidden)
    return sigma * (1.0 + hidden * (1.0 - sigma))


def fill_ids(ids_ref):
    ids_ref[...] = lax.broadcasted_iota(jnp.int32, ids_ref.shape, 0).astype(jnp.float32).astype(jnp.bfloat16)


def one_hot(ids_ref, entries):
    place = (entries & (SPAN - 1)).astype(jnp.float32).astype(jnp.bfloat16)
    return jnp.where(ids_ref[...] == place, jnp.ones((), jnp.bfloat16), jnp.zeros((), jnp.bfloat16))


def over_offsets(offsets, chans, step, unrolled):
    def group(index, carry):
        for inner in range(unrolled):
            k = index * unrolled + inner
            step(k, pl.ds(pl.multiple_of(k * chans, chans), chans))
        return carry

    lax.fori_loop(0, offsets // unrolled, group, 0)


def gather_step(picked_ref, rule_ref, ids_ref, tiles, start, shift):
    chans = tiles[0].shape[0]
    sides = [jnp.concatenate([a, b], 0) for a, b in zip(tiles[:-1], tiles[1:])]

    def step(k, at):
        for q, side in enumerate(sides):
            entries = rule_ref[pl.ds(k, 1), start + SPAN * q : start + SPAN * (q + 1)] - shift
            both = jnp.dot(side, one_hot(ids_ref, entries), preferred_element_type=jnp.float32)
            half = lax.shift_right_arithmetic(entries, 8)
            found = jnp.where(half == q, both[:chans], jnp.where(half == q + 1, both[chans:], 0.0))
            picked_ref[at, SPAN * q : SPAN * (q + 1)] = found.astype(jnp.bfloat16)

    return step


def side_by_side(w_ref, out_ref, turned):
    offsets, chans, _ = w_ref.shape
    for k in range(offsets):
        out_ref[:, k * chans : (k + 1) * chans] = w_ref[k].T if turned else w_ref[k]


def scatter_step(high_ref, low_ref, rule_ref, ids_ref, sources, start, shift):
    chans = sources[0].shape[0]
    last = len(sources) - 1

    def put(at, q, tile):
        first = tile.astype(jnp.bfloat16)
        high_ref[at, SPAN * q : SPAN * (q + 1)] = first
        low_ref[at, SPAN * q : SPAN * (q + 1)] = (tile - first.astype(jnp.float32)).astype(jnp.bfloat16)

    def step(k, at):
        above = None
        for q, source in enumerate(sources):
            entries = rule_ref[pl.ds(k, 1), start + SPAN * q : start + SPAN * (q + 1)] + shift
            half = lax.shift_right_arithmetic(entries, 8)
            none = jnp.zeros((), jnp.bfloat16)
            parts = [] if q == 0 else [jnp.where(half == q, source, none)]
            if q < last:
                parts.append(jnp.where(half == q + 1, source, none))
            spread = lax.dot_general(
                jnp.concatenate(parts, 0) if len(parts) > 1 else parts[0],
                one_hot(ids_ref, entries),
                (((1,), (1,)), ((), ())),
                preferred_element_type=jnp.float32,
            )
            if q > 0:
                put(at, q - 1, above + spread[:chans])
            above = spread[-chans:]

    return step


def through(w_ref, high_ref, low_ref, used):
    total = jnp.dot(w_ref[...], high_ref[:, :used], preferred_element_type=jnp.float32)
    return total + jnp.dot(w_ref[...], low_ref[:, :used], preferred_element_type=jnp.float32)


def pack_kernel(feat_ref, grad_ref, rule_ref, odd_ref, own_ref, to_even_ref, to_odd_ref):
    rows, chans = feat_ref.shape
    offsets = rule_ref.shape[0]
    own_ref[2 * chans :, :] = jnp.zeros((2 * CODE, rows), jnp.bfloat16)
    for b in range(rows // BLOCK):
        at = slice(b * BLOCK, (b + 1) * BLOCK)
        own_ref[:chans, at] = feat_ref[at, :].T
        own_ref[chans : 2 * chans, at] = grad_ref[at, :].T
    entries = rule_ref[...]
    code = jnp.where(entries == rows + 2 * HALO, 0, entries + 1)
    coarse = lax.shift_right_logical(code, 5).astype(jnp.float32).astype(jnp.bfloat16)
    fine = (code & 31).astype(jnp.float32).astype(jnp.bfloat16)
    own_ref[2 * chans : 2 * chans + offsets, :] = coarse
    own_ref[2 * chans + CODE : 2 * chans + CODE + offsets, :] = fine
    first, last = own_ref[:, :EDGE], own_ref[:, rows - EDGE :]
    odd = odd_ref[0] == 1
    to_even_ref[...] = jnp.where(odd, first, last)
    to_odd_ref[...] = jnp.where(odd, last, first)


def grads_kernel(
    own_ref, even_ref, odd_ref, grad_out_ref, w1_ref, w2_ref, core_ref, parity_ref,
    mine_ref, other_ref, source_ref, rule_ref,
    high_ref, low_ref, picked_ref, w_ref, before_ref, after_ref, ids_ref,
):
    rows, chans = grad_out_ref.shape
    offsets = w1_ref.shape[0]
    flat = offsets * chans
    wide = rows + 2 * HALO
    fill_ids(ids_ref)
    mine_ref[flat:, :] = jnp.zeros((mine_ref.shape[0] - flat, chans), jnp.float32)
    other_ref[flat:, :] = jnp.zeros((other_ref.shape[0] - flat, chans), jnp.bfloat16)
    is_odd = parity_ref[0] == 1
    before_ref[...] = jnp.where(is_odd, even_ref[...], odd_ref[...])
    after_ref[...] = jnp.where(is_odd, odd_ref[...], even_ref[...])
    pieces = ((before_ref, -HALO - rows + EDGE), (own_ref, EDGE - HALO), (after_ref, EDGE - HALO + rows))
    column = 0
    for piece, base in pieces:
        coarse = piece[2 * chans : 2 * chans + CODE, :].astype(jnp.float32)
        fine = piece[2 * chans + CODE :, :].astype(jnp.float32)
        code = (coarse * 32.0 + fine).astype(jnp.int32)
        rule_ref[:, column : column + code.shape[1]] = jnp.where(code == 0, NONE, code - 1 + base)
        column += code.shape[1]

    def tiles(top):
        rest = slice(top, top + chans)
        inner = [own_ref[rest, SPAN * p : SPAN * (p + 1)] for p in range(rows // SPAN)]
        return [before_ref[rest, :]] + inner + [after_ref[rest, :]]

    scatter = scatter_step(high_ref, low_ref, rule_ref, ids_ref, tiles(chans), 0, HALO)
    gather = gather_step(picked_ref, rule_ref, ids_ref, tiles(0), HALO, 0)

    def both(k, at):
        scatter(k, at)
        gather(k, at)

    over_offsets(offsets, chans, both, GROUP)
    side_by_side(w2_ref, w_ref, False)
    grad_act = through(w_ref, high_ref, low_ref, wide)
    side_by_side(w1_ref, w_ref, True)
    hidden = jnp.dot(w_ref[...], picked_ref[...], preferred_element_type=jnp.float32)
    act = (hidden * jax.nn.sigmoid(hidden)).astype(jnp.bfloat16)
    grad_hidden = (grad_act * dsilu(hidden)).astype(jnp.bfloat16)
    source_ref[...] = grad_hidden
    inside = slice(HALO, HALO + rows)
    first = lax.dot_general(
        picked_ref[:, inside], grad_hidden[:, inside], (((1,), (1,)), ((), ())), preferred_element_type=jnp.float32
    )

    @pl.when(core_ref[0] == 0)
    def _():
        mine_ref[:flat, :] = first

    @pl.when(core_ref[0] != 0)
    def _():
        other_ref[:flat, :] = first.astype(jnp.bfloat16)

    act_tiles = [act[:, SPAN * q : SPAN * (q + 1)] for q in range(wide // SPAN)]
    gather = gather_step(high_ref, rule_ref, ids_ref, act_tiles, EDGE, EDGE - HALO)
    over_offsets(offsets, chans, gather, LONG)
    second = jnp.dot(high_ref[:, :rows], grad_out_ref[...], preferred_element_type=jnp.float32)

    @pl.when(core_ref[0] != 0)
    def _():
        mine_ref[:flat, :] = second

    @pl.when(core_ref[0] == 0)
    def _():
        other_ref[:flat, :] = second.astype(jnp.bfloat16)


def input_grad_kernel(
    source_ref, rule_ref, w1_ref, grad_out_ref, live_ref, out_ref, high_ref, low_ref, w_ref, ids_ref
):
    rows, chans = grad_out_ref.shape
    offsets = w1_ref.shape[0]
    fill_ids(ids_ref)
    side_by_side(w1_ref, w_ref, False)
    sources = [source_ref[:, SPAN * q : SPAN * (q + 1)] for q in range(source_ref.shape[1] // SPAN)]
    scatter = scatter_step(high_ref, low_ref, rule_ref, ids_ref, sources, HALO, 0)
    over_offsets(offsets, chans, scatter, LONG)
    total = through(w_ref, high_ref, low_ref, rows)
    for b in range(rows // BLOCK):
        at = slice(b * BLOCK, (b + 1) * BLOCK)
        added = grad_out_ref[at, :].astype(jnp.float32) + total[:, at].T
        out_ref[at, :] = (live_ref[b].astype(jnp.float32) * added).astype(jnp.bfloat16)


def call(kernel, outs, scratch, *args, scalars=0, flops=0):
    vmem = pl.BlockSpec(memory_space=pltpu.VMEM)
    smem = pl.BlockSpec(memory_space=pltpu.SMEM)
    shapes = [jax.ShapeDtypeStruct(shape, dtype) for shape, dtype in outs]
    moved = sum(x.size * x.dtype.itemsize for x in (*args, *shapes))
    return pl.pallas_call(
        kernel,
        out_shape=shapes,
        in_specs=[vmem] * (len(args) - scalars) + [smem] * scalars,
        out_specs=[vmem] * len(outs),
        scratch_shapes=[pltpu.VMEM(shape, dtype) for shape, dtype in scratch],
        cost_estimate=pl.CostEstimate(flops=flops, bytes_accessed=moved, transcendentals=0),
    )(*args)


def on_device(features, grad_out, w1, w2, rulebook, live_blocks):
    rows, chans = features.shape
    offsets = w1.shape[0]
    wide = rows + 2 * HALO
    flat = offsets * chans
    padded = flat + chans
    bf16, f32, i32 = (jnp.bfloat16, jnp.float32, jnp.int32)
    ids = ((SPAN, SPAN), bf16)
    spread = ((flat, wide), bf16)
    beside = ((chans, flat), bf16)
    tall = 2 * chans + 2 * CODE
    one_pass = 2 * offsets * rows * SPAN * SPAN
    parity = (lax.axis_index("x").astype(i32) & 1).reshape(1)
    own, to_even, to_odd = call(
        pack_kernel,
        [((tall, rows), bf16), ((tall, EDGE), bf16), ((tall, EDGE), bf16)],
        [],
        features,
        grad_out,
        rulebook,
        parity,
        scalars=1,
    )
    odd = swapped(to_odd, BLOCKS, 1)
    even = swapped(to_even, BLOCKS, 0)
    core = lax.axis_index("core").astype(i32).reshape(1)
    mine, other, grad_hidden, wide_rules = call(
        grads_kernel,
        [((padded, chans), f32), ((padded, chans), bf16), ((chans, wide), bf16), ((CODE, rows + 2 * EDGE), i32)],
        [spread, spread, spread, beside, ((tall, EDGE), bf16), ((tall, EDGE), bf16), ids],
        own,
        even,
        odd,
        grad_out,
        w1,
        w2,
        core,
        parity,
        scalars=2,
        flops=6 * one_pass,
    )
    (grad_in,) = call(
        input_grad_kernel,
        [((rows, chans), bf16)],
        [((flat, rows), bf16), ((flat, rows), bf16), beside, ids],
        grad_hidden,
        wide_rules,
        w1,
        grad_out,
        live_blocks,
        scalars=1,
        flops=2 * one_pass,
    )
    kern_one, kern_two = reduce_everywhere(mine, other)
    voxel_total = rows * lax.axis_size(REGIONS) * lax.axis_size(BLOCKS)
    scale = jnp.sqrt(jnp.float32(voxel_total))
    return (grad_in, kern_one[:flat].reshape(w1.shape) / scale, kern_two[:flat].reshape(w1.shape) / scale)


def solution(mesh):
    rows = P(REGIONS + BLOCKS)

    return jax.shard_map(
        on_device,
        mesh=fine_mesh(mesh),
        in_specs=(rows, rows, P(), P(), P(None, REGIONS + BLOCKS), rows),
        out_specs=(rows, P(), P()),
        check_vma=False,
    )
```

```python
import jax
import jax.numpy as jnp
from jax import lax
from jax.experimental import pallas as pl
from jax.experimental.pallas import tpu as pltpu
from jax.sharding import Mesh, PartitionSpec as P

BLOCK = 128
HALO = 128
SPAN = 256
EDGE = 256
CODE = 32
NONE = 4096
GROUP = 9
LONG = 9


def swapped(x, axis, odd):
    length = lax.axis_size(axis)
    pairs = [(i, ((i + odd) ^ 1) - odd) for i in range(length)]
    return lax.ppermute(x, axis, [(i, j) for i, j in pairs if 0 <= j < length])


SWAP = [(0, 1), (1, 0)]
PLANE = ("yh", "yl", "z_lo", "x")
BLOCKS = ("yl", "z_hi", "z_lo", "x")
REGIONS = ("yh", "core")


def fine_mesh(mesh):
    return Mesh(mesh.devices.reshape(2, 2, 2, 4, 2, 4), ("yh", "core", "yl", "z_hi", "z_lo", "x"))


def reduce_everywhere(own, other):
    core = lax.axis_index("core")
    lanes = own.shape[1]
    own = own + lax.ppermute(other, "core", SWAP).astype(jnp.float32)
    count = lax.axis_size(PLANE)
    parts = own.astype(jnp.bfloat16).reshape(count, -1, lanes)
    parts = lax.all_to_all(parts, PLANE, 0, 0, tiled=True)
    own = parts.astype(jnp.float32).sum(0)
    for flip in (1, 3):
        own = own + lax.ppermute(own, "z_hi", [(i, i ^ flip) for i in range(lax.axis_size("z_hi"))])
    parts = jnp.broadcast_to(own.astype(jnp.bfloat16)[None], (count,) + own.shape)
    parts = lax.all_to_all(parts, PLANE, 0, 0, tiled=True).reshape(-1, lanes)
    other = lax.ppermute(parts, "core", SWAP)
    first = jnp.where(core == 0, parts, other)
    second = jnp.where(core == 0, other, parts)
    return first.astype(jnp.float32), second.astype(jnp.float32)


def dsilu(hidden):
    sigma = jax.nn.sigmoid(hidden)
    return sigma * (1.0 + hidden * (1.0 - sigma))


def fill_ids(ids_ref):
    ids_ref[...] = lax.broadcasted_iota(jnp.int32, ids_ref.shape, 0).astype(jnp.float32).astype(jnp.bfloat16)


def one_hot(ids_ref, entries):
    place = (entries & (SPAN - 1)).astype(jnp.float32).astype(jnp.bfloat16)
    return jnp.where(ids_ref[...] == place, jnp.ones((), jnp.bfloat16), jnp.zeros((), jnp.bfloat16))


def over_offsets(offsets, chans, step, unrolled):
    def group(index, carry):
        for inner in range(unrolled):
            k = index * unrolled + inner
            step(k, pl.ds(pl.multiple_of(k * chans, chans), chans))
        return carry

    lax.fori_loop(0, offsets // unrolled, group, 0)


def gather_step(picked_ref, rule_ref, ids_ref, tiles, start, shift, groups=None):
    chans = tiles[0].shape[0]
    groups = range(len(tiles) - 1) if groups is None else groups
    sides = [jnp.concatenate([tiles[q], tiles[q + 1]], 0) for q in groups]

    def step(k, at):
        for slot, (q, side) in enumerate(zip(groups, sides)):
            entries = rule_ref[pl.ds(k, 1), start + SPAN * q : start + SPAN * (q + 1)] - shift
            both = jnp.dot(side, one_hot(ids_ref, entries), preferred_element_type=jnp.float32)
            half = lax.shift_right_arithmetic(entries, 8)
            found = jnp.where(half == q, both[:chans], jnp.where(half == q + 1, both[chans:], 0.0))
            picked_ref[at, SPAN * slot : SPAN * (slot + 1)] = found.astype(jnp.bfloat16)

    return step


def side_by_side(w_ref, out_ref, turned):
    offsets, chans, _ = w_ref.shape
    for k in range(offsets):
        out_ref[:, k * chans : (k + 1) * chans] = w_ref[k].T if turned else w_ref[k]


def scatter_step(high_ref, low_ref, rule_ref, ids_ref, sources, start, shift):
    chans = sources[0].shape[0]
    last = len(sources) - 1

    def put(at, q, tile):
        first = tile.astype(jnp.bfloat16)
        high_ref[at, SPAN * q : SPAN * (q + 1)] = first
        low_ref[at, SPAN * q : SPAN * (q + 1)] = (tile - first.astype(jnp.float32)).astype(jnp.bfloat16)

    def step(k, at):
        above = None
        for q, source in enumerate(sources):
            entries = rule_ref[pl.ds(k, 1), start + SPAN * q : start + SPAN * (q + 1)] + shift
            half = lax.shift_right_arithmetic(entries, 8)
            none = jnp.zeros((), jnp.bfloat16)
            parts = [] if q == 0 else [jnp.where(half == q, source, none)]
            if q < last:
                parts.append(jnp.where(half == q + 1, source, none))
            spread = lax.dot_general(
                jnp.concatenate(parts, 0) if len(parts) > 1 else parts[0],
                one_hot(ids_ref, entries),
                (((1,), (1,)), ((), ())),
                preferred_element_type=jnp.float32,
            )
            if q > 0:
                put(at, q - 1, above + spread[:chans])
            above = spread[-chans:]

    return step


def through(w_ref, high_ref, low_ref, used):
    total = jnp.dot(w_ref[...], high_ref[:, :used], preferred_element_type=jnp.float32)
    return total + jnp.dot(w_ref[...], low_ref[:, :used], preferred_element_type=jnp.float32)


def pack_kernel(feat_ref, grad_ref, rule_ref, odd_ref, own_ref, to_even_ref, to_odd_ref):
    rows, chans = feat_ref.shape
    offsets = rule_ref.shape[0]
    own_ref[2 * chans :, :] = jnp.zeros((2 * CODE, rows), jnp.bfloat16)
    for b in range(rows // BLOCK):
        at = slice(b * BLOCK, (b + 1) * BLOCK)
        own_ref[:chans, at] = feat_ref[at, :].T
        own_ref[chans : 2 * chans, at] = grad_ref[at, :].T
    entries = rule_ref[...]
    code = jnp.where(entries == rows + 2 * HALO, 0, entries + 1)
    coarse = lax.shift_right_logical(code, 5).astype(jnp.float32).astype(jnp.bfloat16)
    fine = (code & 31).astype(jnp.float32).astype(jnp.bfloat16)
    own_ref[2 * chans : 2 * chans + offsets, :] = coarse
    own_ref[2 * chans + CODE : 2 * chans + CODE + offsets, :] = fine
    first, last = own_ref[:, :EDGE], own_ref[:, rows - EDGE :]
    odd = odd_ref[0] == 1
    to_even_ref[...] = jnp.where(odd, first, last)
    to_odd_ref[...] = jnp.where(odd, last, first)


def wide_entries(piece, chans, base):
    coarse = piece[2 * chans : 2 * chans + CODE, :].astype(jnp.float32)
    fine = piece[2 * chans + CODE :, :].astype(jnp.float32)
    code = (coarse * 32.0 + fine).astype(jnp.int32)
    return jnp.where(code == 0, NONE, code - 1 + base)


def early_kernel(own_ref, picked_ref, rule_ref, ids_ref):
    flat, _ = picked_ref.shape
    rows = own_ref.shape[1]
    chans = (own_ref.shape[0] - 2 * CODE) // 2
    fill_ids(ids_ref)
    rule_ref[...] = wide_entries(own_ref, chans, -HALO)
    inner = [own_ref[:chans, SPAN * p : SPAN * (p + 1)] for p in range(rows // SPAN)]
    gather = gather_step(picked_ref, rule_ref, ids_ref, inner, HALO, 0)
    over_offsets(flat // chans, chans, gather, LONG)


def grads_kernel(
    own_ref, even_ref, odd_ref, grad_out_ref, w1_ref, w2_ref, early_ref, core_ref, parity_ref,
    mine_ref, other_ref, source_ref, rule_ref,
    high_ref, low_ref, edge_ref, middle_ref, w_ref, before_ref, after_ref, ids_ref, sem,
):
    rows, chans = grad_out_ref.shape
    offsets = w1_ref.shape[0]
    flat = offsets * chans
    wide = rows + 2 * HALO
    arriving = pltpu.make_async_copy(early_ref, middle_ref, sem)
    arriving.start()
    fill_ids(ids_ref)
    mine_ref[flat:, :] = jnp.zeros((mine_ref.shape[0] - flat, chans), jnp.float32)
    other_ref[flat:, :] = jnp.zeros((other_ref.shape[0] - flat, chans), jnp.bfloat16)
    is_odd = parity_ref[0] == 1
    before_ref[...] = jnp.where(is_odd, even_ref[...], odd_ref[...])
    after_ref[...] = jnp.where(is_odd, odd_ref[...], even_ref[...])
    pieces = ((before_ref, -HALO - rows + EDGE), (own_ref, EDGE - HALO), (after_ref, EDGE - HALO + rows))
    column = 0
    for piece, base in pieces:
        entries = wide_entries(piece, chans, base)
        rule_ref[:, column : column + entries.shape[1]] = entries
        column += entries.shape[1]

    def tiles(top):
        rest = slice(top, top + chans)
        inner = [own_ref[rest, SPAN * p : SPAN * (p + 1)] for p in range(rows // SPAN)]
        return [before_ref[rest, :]] + inner + [after_ref[rest, :]]

    scatter = scatter_step(high_ref, low_ref, rule_ref, ids_ref, tiles(chans), 0, HALO)
    ends = (0, wide // SPAN - 1)
    gather = gather_step(edge_ref, rule_ref, ids_ref, tiles(0), HALO, 0, ends)

    def both(k, at):
        scatter(k, at)
        gather(k, at)

    over_offsets(offsets, chans, both, GROUP)
    side_by_side(w2_ref, w_ref, False)
    grad_act = through(w_ref, high_ref, low_ref, wide)
    side_by_side(w1_ref, w_ref, True)
    arriving.wait()
    ended = jnp.dot(w_ref[...], edge_ref[...], preferred_element_type=jnp.float32)
    middle = jnp.dot(w_ref[...], middle_ref[...], preferred_element_type=jnp.float32)
    hidden = jnp.concatenate([ended[:, :SPAN], middle, ended[:, SPAN:]], 1)
    act = (hidden * jax.nn.sigmoid(hidden)).astype(jnp.bfloat16)
    grad_hidden = (grad_act * dsilu(hidden)).astype(jnp.bfloat16)
    source_ref[...] = grad_hidden
    outer = jnp.concatenate([grad_hidden[:, HALO:SPAN], grad_hidden[:, wide - SPAN : wide - HALO]], 1)
    across = (((1,), (1,)), ((), ()))
    first = lax.dot_general(
        middle_ref[...], grad_hidden[:, SPAN : wide - SPAN], across, preferred_element_type=jnp.float32
    ) + lax.dot_general(edge_ref[:, HALO : SPAN + HALO], outer, across, preferred_element_type=jnp.float32)

    @pl.when(core_ref[0] == 0)
    def _():
        mine_ref[:flat, :] = first

    @pl.when(core_ref[0] != 0)
    def _():
        other_ref[:flat, :] = first.astype(jnp.bfloat16)

    act_tiles = [act[:, SPAN * q : SPAN * (q + 1)] for q in range(wide // SPAN)]
    gather = gather_step(high_ref, rule_ref, ids_ref, act_tiles, EDGE, EDGE - HALO)
    over_offsets(offsets, chans, gather, LONG)
    second = jnp.dot(high_ref[:, :rows], grad_out_ref[...], preferred_element_type=jnp.float32)

    @pl.when(core_ref[0] != 0)
    def _():
        mine_ref[:flat, :] = second

    @pl.when(core_ref[0] == 0)
    def _():
        other_ref[:flat, :] = second.astype(jnp.bfloat16)


def input_grad_kernel(
    source_ref, rule_ref, w1_ref, grad_out_ref, live_ref, out_ref, high_ref, low_ref, w_ref, ids_ref
):
    rows, chans = grad_out_ref.shape
    offsets = w1_ref.shape[0]
    fill_ids(ids_ref)
    side_by_side(w1_ref, w_ref, False)
    sources = [source_ref[:, SPAN * q : SPAN * (q + 1)] for q in range(source_ref.shape[1] // SPAN)]
    scatter = scatter_step(high_ref, low_ref, rule_ref, ids_ref, sources, HALO, 0)
    over_offsets(offsets, chans, scatter, LONG)
    total = through(w_ref, high_ref, low_ref, rows)
    for b in range(rows // BLOCK):
        at = slice(b * BLOCK, (b + 1) * BLOCK)
        added = grad_out_ref[at, :].astype(jnp.float32) + total[:, at].T
        out_ref[at, :] = (live_ref[b].astype(jnp.float32) * added).astype(jnp.bfloat16)


def call(kernel, outs, scratch, *args, scalars=0, held=0, flops=0):
    vmem = pl.BlockSpec(memory_space=pltpu.VMEM)
    hbm = pl.BlockSpec(memory_space=pl.ANY)
    smem = pl.BlockSpec(memory_space=pltpu.SMEM)
    shapes = [jax.ShapeDtypeStruct(shape, dtype) for shape, dtype in outs]
    moved = sum(x.size * x.dtype.itemsize for x in (*args, *shapes))
    return pl.pallas_call(
        kernel,
        out_shape=shapes,
        in_specs=[vmem] * (len(args) - scalars - held) + [hbm] * held + [smem] * scalars,
        out_specs=[vmem] * len(outs),
        scratch_shapes=[pltpu.VMEM(*kind) for kind in scratch] + [pltpu.SemaphoreType.DMA] * held,
        cost_estimate=pl.CostEstimate(flops=flops, bytes_accessed=moved, transcendentals=0),
    )(*args)


def on_device(features, grad_out, w1, w2, rulebook, live_blocks):
    rows, chans = features.shape
    offsets = w1.shape[0]
    wide = rows + 2 * HALO
    flat = offsets * chans
    padded = flat + chans
    bf16, f32, i32 = (jnp.bfloat16, jnp.float32, jnp.int32)
    ids = ((SPAN, SPAN), bf16)
    spread = ((flat, wide), bf16)
    half = ((flat, wide - 2 * SPAN), bf16)
    beside = ((chans, flat), bf16)
    tall = 2 * chans + 2 * CODE
    one_pass = 2 * offsets * rows * SPAN * SPAN
    parity = (lax.axis_index("x").astype(i32) & 1).reshape(1)
    own, to_even, to_odd = call(
        pack_kernel,
        [((tall, rows), bf16), ((tall, EDGE), bf16), ((tall, EDGE), bf16)],
        [],
        features,
        grad_out,
        rulebook,
        parity,
        scalars=1,
    )
    even = swapped(to_even, BLOCKS, 0)
    odd = swapped(to_odd, BLOCKS, 1)
    (early,) = call(early_kernel, [((flat, wide - 2 * SPAN), bf16)], [((CODE, rows), i32), ids], own, flops=one_pass)
    core = lax.axis_index("core").astype(i32).reshape(1)
    mine, other, grad_hidden, wide_rules = call(
        grads_kernel,
        [((padded, chans), f32), ((padded, chans), bf16), ((chans, wide), bf16), ((CODE, rows + 2 * EDGE), i32)],
        [spread, spread, half, half, beside, ((tall, EDGE), bf16), ((tall, EDGE), bf16), ids],
        own,
        even,
        odd,
        grad_out,
        w1,
        w2,
        early,
        core,
        parity,
        scalars=2,
        held=1,
        flops=6 * one_pass,
    )
    (grad_in,) = call(
        input_grad_kernel,
        [((rows, chans), bf16)],
        [((flat, rows), bf16), ((flat, rows), bf16), beside, ids],
        grad_hidden,
        wide_rules,
        w1,
        grad_out,
        live_blocks,
        scalars=1,
        flops=2 * one_pass,
    )
    kern_one, kern_two = reduce_everywhere(mine, other)
    voxel_total = rows * lax.axis_size(REGIONS) * lax.axis_size(BLOCKS)
    scale = jnp.sqrt(jnp.float32(voxel_total))
    return (grad_in, kern_one[:flat].reshape(w1.shape) / scale, kern_two[:flat].reshape(w1.shape) / scale)


def solution(mesh):
    rows = P(REGIONS + BLOCKS)

    return jax.shard_map(
        on_device,
        mesh=fine_mesh(mesh),
        in_specs=(rows, rows, P(), P(), P(None, REGIONS + BLOCKS), rows),
        out_specs=(rows, P(), P()),
        check_vma=False,
    )
```

```python
import jax
import jax.numpy as jnp
from jax import lax
from jax.experimental import pallas as pl
from jax.experimental.pallas import tpu as pltpu
from jax.sharding import Mesh, PartitionSpec as P

BLOCK = 128
HALO = 128
SPAN = 256
EDGE = 256
CODE = 32
NONE = 4096
GROUP = 9
LONG = 9


def swapped(x, axis, odd):
    length = lax.axis_size(axis)
    pairs = [(i, ((i + odd) ^ 1) - odd) for i in range(length)]
    return lax.ppermute(x, axis, [(i, j) for i, j in pairs if 0 <= j < length])


SWAP = [(0, 1), (1, 0)]
PLANE = ("yh", "yl", "z_lo", "x")
BLOCKS = ("yl", "z_hi", "z_lo", "x")
REGIONS = ("yh", "core")


def fine_mesh(mesh):
    return Mesh(mesh.devices.reshape(2, 2, 2, 4, 2, 4), ("yh", "core", "yl", "z_hi", "z_lo", "x"))


def reduce_everywhere(own, other):
    core = lax.axis_index("core")
    lanes = own.shape[1]
    own = own + lax.ppermute(other, "core", SWAP).astype(jnp.float32)
    count = lax.axis_size(PLANE)
    parts = own.astype(jnp.bfloat16).reshape(count, -1, lanes)
    parts = lax.all_to_all(parts, PLANE, 0, 0, tiled=True)
    own = parts.astype(jnp.float32).sum(0)
    for flip in (1, 3):
        own = own + lax.ppermute(own, "z_hi", [(i, i ^ flip) for i in range(lax.axis_size("z_hi"))])
    parts = jnp.broadcast_to(own.astype(jnp.bfloat16)[None], (count,) + own.shape)
    parts = lax.all_to_all(parts, PLANE, 0, 0, tiled=True).reshape(-1, lanes)
    other = lax.ppermute(parts, "core", SWAP)
    first = jnp.where(core == 0, parts, other)
    second = jnp.where(core == 0, other, parts)
    return first.astype(jnp.float32), second.astype(jnp.float32)


def dsilu(hidden):
    sigma = jax.nn.sigmoid(hidden)
    return sigma * (1.0 + hidden * (1.0 - sigma))


def fill_ids(ids_ref):
    ids_ref[...] = lax.broadcasted_iota(jnp.int32, ids_ref.shape, 0).astype(jnp.float32).astype(jnp.bfloat16)


def one_hot(ids_ref, entries):
    place = (entries & (SPAN - 1)).astype(jnp.float32).astype(jnp.bfloat16)
    return jnp.where(ids_ref[...] == place, jnp.ones((), jnp.bfloat16), jnp.zeros((), jnp.bfloat16))


def over_offsets(offsets, chans, step, unrolled):
    def group(index, carry):
        for inner in range(unrolled):
            k = index * unrolled + inner
            step(k, pl.ds(pl.multiple_of(k * chans, chans), chans))
        return carry

    lax.fori_loop(0, offsets // unrolled, group, 0)


def gather_step(picked_ref, rule_ref, ids_ref, tiles, start, shift):
    chans = tiles[0].shape[0]
    sides = [jnp.concatenate([a, b], 0) for a, b in zip(tiles[:-1], tiles[1:])]

    def step(k, at):
        for q, side in enumerate(sides):
            entries = rule_ref[pl.ds(k, 1), start + SPAN * q : start + SPAN * (q + 1)] - shift
            both = jnp.dot(side, one_hot(ids_ref, entries), preferred_element_type=jnp.float32)
            half = lax.shift_right_arithmetic(entries, 8)
            found = jnp.where(half == q, both[:chans], jnp.where(half == q + 1, both[chans:], 0.0))
            picked_ref[at, SPAN * q : SPAN * (q + 1)] = found.astype(jnp.bfloat16)

    return step


def side_by_side(w_ref, out_ref, turned):
    offsets, chans, _ = w_ref.shape
    for k in range(offsets):
        out_ref[:, k * chans : (k + 1) * chans] = w_ref[k].T if turned else w_ref[k]


def scatter_step(high_ref, low_ref, rule_ref, ids_ref, sources, start, shift):
    chans = sources[0].shape[0]
    last = len(sources) - 1

    def put(at, q, tile):
        first = tile.astype(jnp.bfloat16)
        high_ref[at, SPAN * q : SPAN * (q + 1)] = first
        low_ref[at, SPAN * q : SPAN * (q + 1)] = (tile - first.astype(jnp.float32)).astype(jnp.bfloat16)

    def step(k, at):
        above = None
        for q, source in enumerate(sources):
            entries = rule_ref[pl.ds(k, 1), start + SPAN * q : start + SPAN * (q + 1)] + shift
            half = lax.shift_right_arithmetic(entries, 8)
            none = jnp.zeros((), jnp.bfloat16)
            parts = [] if q == 0 else [jnp.where(half == q, source, none)]
            if q < last:
                parts.append(jnp.where(half == q + 1, source, none))
            spread = lax.dot_general(
                jnp.concatenate(parts, 0) if len(parts) > 1 else parts[0],
                one_hot(ids_ref, entries),
                (((1,), (1,)), ((), ())),
                preferred_element_type=jnp.float32,
            )
            if q > 0:
                put(at, q - 1, above + spread[:chans])
            above = spread[-chans:]

    return step


def through(w_ref, high_ref, low_ref, used):
    total = jnp.dot(w_ref[...], high_ref[:, :used], preferred_element_type=jnp.float32)
    return total + jnp.dot(w_ref[...], low_ref[:, :used], preferred_element_type=jnp.float32)


def pack_rows(out_ref, feat_ref, grad_ref, rule_ref, start):
    rows, chans = feat_ref.shape
    offsets = rule_ref.shape[0]
    count = out_ref.shape[1]
    out_ref[2 * chans :, :] = jnp.zeros((2 * CODE, count), jnp.bfloat16)
    for b in range(count // BLOCK):
        at = slice(b * BLOCK, (b + 1) * BLOCK)
        source = slice(start + b * BLOCK, start + (b + 1) * BLOCK)
        out_ref[:chans, at] = feat_ref[source, :].T
        out_ref[chans : 2 * chans, at] = grad_ref[source, :].T
    entries = rule_ref[:, start : start + count]
    code = jnp.where(entries == rows + 2 * HALO, 0, entries + 1)
    coarse = lax.shift_right_logical(code, 5).astype(jnp.float32).astype(jnp.bfloat16)
    fine = (code & 31).astype(jnp.float32).astype(jnp.bfloat16)
    out_ref[2 * chans : 2 * chans + offsets, :] = coarse
    out_ref[2 * chans + CODE : 2 * chans + CODE + offsets, :] = fine


def edges_kernel(feat_ref, grad_ref, rule_ref, odd_ref, to_even_ref, to_odd_ref):
    last = feat_ref.shape[0] - EDGE

    @pl.when(odd_ref[0] == 1)
    def _():
        pack_rows(to_even_ref, feat_ref, grad_ref, rule_ref, 0)
        pack_rows(to_odd_ref, feat_ref, grad_ref, rule_ref, last)

    @pl.when(odd_ref[0] != 1)
    def _():
        pack_rows(to_even_ref, feat_ref, grad_ref, rule_ref, last)
        pack_rows(to_odd_ref, feat_ref, grad_ref, rule_ref, 0)


def own_kernel(feat_ref, grad_ref, rule_ref, own_ref):
    pack_rows(own_ref, feat_ref, grad_ref, rule_ref, 0)


def grads_kernel(
    own_ref, even_ref, odd_ref, grad_out_hbm, w1_hbm, w2_hbm, core_ref, parity_ref,
    mine_ref, other_ref, source_ref, rule_ref,
    high_ref, low_ref, picked_ref, w_ref, before_ref, after_ref, ids_ref,
    grad_out_ref, w1_ref, w2_ref, grad_out_sem, w1_sem, w2_sem,
):
    rows, chans = grad_out_ref.shape
    offsets = w1_ref.shape[0]
    flat = offsets * chans
    wide = rows + 2 * HALO
    arriving = [
        pltpu.make_async_copy(grad_out_hbm, grad_out_ref, grad_out_sem),
        pltpu.make_async_copy(w1_hbm, w1_ref, w1_sem),
        pltpu.make_async_copy(w2_hbm, w2_ref, w2_sem),
    ]
    for copy in arriving:
        copy.start()
    fill_ids(ids_ref)
    mine_ref[flat:, :] = jnp.zeros((mine_ref.shape[0] - flat, chans), jnp.float32)
    other_ref[flat:, :] = jnp.zeros((other_ref.shape[0] - flat, chans), jnp.bfloat16)
    is_odd = parity_ref[0] == 1
    before_ref[...] = jnp.where(is_odd, even_ref[...], odd_ref[...])
    after_ref[...] = jnp.where(is_odd, odd_ref[...], even_ref[...])
    pieces = ((before_ref, -HALO - rows + EDGE), (own_ref, EDGE - HALO), (after_ref, EDGE - HALO + rows))
    column = 0
    for piece, base in pieces:
        coarse = piece[2 * chans : 2 * chans + CODE, :].astype(jnp.float32)
        fine = piece[2 * chans + CODE :, :].astype(jnp.float32)
        code = (coarse * 32.0 + fine).astype(jnp.int32)
        rule_ref[:, column : column + code.shape[1]] = jnp.where(code == 0, NONE, code - 1 + base)
        column += code.shape[1]

    def tiles(top):
        rest = slice(top, top + chans)
        inner = [own_ref[rest, SPAN * p : SPAN * (p + 1)] for p in range(rows // SPAN)]
        return [before_ref[rest, :]] + inner + [after_ref[rest, :]]

    scatter = scatter_step(high_ref, low_ref, rule_ref, ids_ref, tiles(chans), 0, HALO)
    gather = gather_step(picked_ref, rule_ref, ids_ref, tiles(0), HALO, 0)

    def both(k, at):
        scatter(k, at)
        gather(k, at)

    over_offsets(offsets, chans, both, GROUP)
    for copy in arriving:
        copy.wait()
    side_by_side(w2_ref, w_ref, False)
    grad_act = through(w_ref, high_ref, low_ref, wide)
    side_by_side(w1_ref, w_ref, True)
    hidden = jnp.dot(w_ref[...], picked_ref[...], preferred_element_type=jnp.float32)
    act = (hidden * jax.nn.sigmoid(hidden)).astype(jnp.bfloat16)
    grad_hidden = (grad_act * dsilu(hidden)).astype(jnp.bfloat16)
    source_ref[...] = grad_hidden
    inside = slice(HALO, HALO + rows)
    first = lax.dot_general(
        picked_ref[:, inside], grad_hidden[:, inside], (((1,), (1,)), ((), ())), preferred_element_type=jnp.float32
    )

    @pl.when(core_ref[0] == 0)
    def _():
        mine_ref[:flat, :] = first

    @pl.when(core_ref[0] != 0)
    def _():
        other_ref[:flat, :] = first.astype(jnp.bfloat16)

    act_tiles = [act[:, SPAN * q : SPAN * (q + 1)] for q in range(wide // SPAN)]
    gather = gather_step(high_ref, rule_ref, ids_ref, act_tiles, EDGE, EDGE - HALO)
    over_offsets(offsets, chans, gather, LONG)
    second = jnp.dot(high_ref[:, :rows], grad_out_ref[...], preferred_element_type=jnp.float32)

    @pl.when(core_ref[0] != 0)
    def _():
        mine_ref[:flat, :] = second

    @pl.when(core_ref[0] == 0)
    def _():
        other_ref[:flat, :] = second.astype(jnp.bfloat16)


def input_grad_kernel(
    source_ref, rule_ref, w1_ref, grad_out_ref, live_ref, out_ref, high_ref, low_ref, w_ref, ids_ref
):
    rows, chans = grad_out_ref.shape
    offsets = w1_ref.shape[0]
    fill_ids(ids_ref)
    side_by_side(w1_ref, w_ref, False)
    sources = [source_ref[:, SPAN * q : SPAN * (q + 1)] for q in range(source_ref.shape[1] // SPAN)]
    scatter = scatter_step(high_ref, low_ref, rule_ref, ids_ref, sources, HALO, 0)
    over_offsets(offsets, chans, scatter, LONG)
    total = through(w_ref, high_ref, low_ref, rows)
    for b in range(rows // BLOCK):
        at = slice(b * BLOCK, (b + 1) * BLOCK)
        added = grad_out_ref[at, :].astype(jnp.float32) + total[:, at].T
        out_ref[at, :] = (live_ref[b].astype(jnp.float32) * added).astype(jnp.bfloat16)


def call(kernel, outs, scratch, *args, scalars=0, held=0, flops=0):
    vmem = pl.BlockSpec(memory_space=pltpu.VMEM)
    hbm = pl.BlockSpec(memory_space=pl.ANY)
    smem = pl.BlockSpec(memory_space=pltpu.SMEM)
    shapes = [jax.ShapeDtypeStruct(shape, dtype) for shape, dtype in outs]
    moved = sum(x.size * x.dtype.itemsize for x in (*args, *shapes))
    return pl.pallas_call(
        kernel,
        out_shape=shapes,
        in_specs=[vmem] * (len(args) - scalars - held) + [hbm] * held + [smem] * scalars,
        out_specs=[vmem] * len(outs),
        scratch_shapes=[pltpu.VMEM(*kind) for kind in scratch] + [pltpu.SemaphoreType.DMA] * held,
        cost_estimate=pl.CostEstimate(flops=flops, bytes_accessed=moved, transcendentals=0),
    )(*args)


def on_device(features, grad_out, w1, w2, rulebook, live_blocks):
    rows, chans = features.shape
    offsets = w1.shape[0]
    wide = rows + 2 * HALO
    flat = offsets * chans
    padded = flat + chans
    bf16, f32, i32 = (jnp.bfloat16, jnp.float32, jnp.int32)
    ids = ((SPAN, SPAN), bf16)
    spread = ((flat, wide), bf16)
    beside = ((chans, flat), bf16)
    tall = 2 * chans + 2 * CODE
    one_pass = 2 * offsets * rows * SPAN * SPAN
    parity = (lax.axis_index("x").astype(i32) & 1).reshape(1)
    edge = ((tall, EDGE), bf16)
    to_even, to_odd = call(edges_kernel, [edge, edge], [], features, grad_out, rulebook, parity, scalars=1)
    (own,) = call(own_kernel, [((tall, rows), bf16)], [], features, grad_out, rulebook)
    even = swapped(to_even, BLOCKS, 0)
    odd = swapped(to_odd, BLOCKS, 1)
    core = lax.axis_index("core").astype(i32).reshape(1)
    mine, other, grad_hidden, wide_rules = call(
        grads_kernel,
        [((padded, chans), f32), ((padded, chans), bf16), ((chans, wide), bf16), ((CODE, rows + 2 * EDGE), i32)],
        [spread, spread, spread, beside, edge, edge, ids, (grad_out.shape, bf16), (w1.shape, bf16), (w2.shape, bf16)],
        own,
        even,
        odd,
        grad_out,
        w1,
        w2,
        core,
        parity,
        scalars=2,
        held=3,
        flops=6 * one_pass,
    )
    (grad_in,) = call(
        input_grad_kernel,
        [((rows, chans), bf16)],
        [((flat, rows), bf16), ((flat, rows), bf16), beside, ids],
        grad_hidden,
        wide_rules,
        w1,
        grad_out,
        live_blocks,
        scalars=1,
        flops=2 * one_pass,
    )
    kern_one, kern_two = reduce_everywhere(mine, other)
    voxel_total = rows * lax.axis_size(REGIONS) * lax.axis_size(BLOCKS)
    scale = jnp.sqrt(jnp.float32(voxel_total))
    return (grad_in, kern_one[:flat].reshape(w1.shape) / scale, kern_two[:flat].reshape(w1.shape) / scale)


def solution(mesh):
    rows = P(REGIONS + BLOCKS)

    return jax.shard_map(
        on_device,
        mesh=fine_mesh(mesh),
        in_specs=(rows, rows, P(), P(), P(None, REGIONS + BLOCKS), rows),
        out_specs=(rows, P(), P()),
        check_vma=False,
    )
```
